512 devices in a mesh: req: 128 (over x, y_lo, z), tp: 4 (over y_hi, core).
Axes of the slice: x: 4, y: 8 (y_hi: 2, y_lo: 4; y = y_hi * 4 + y_lo), z: 8, core: 2. Of those that a mesh axis runs over, the one named last changes fastest.
Arguments:
- tokens: bfloat16 [32768, 2048], P('req', 'tp'), may hold values from -1100 to 1100
- norm_gain: bfloat16 [2048], replicated, may hold values from 0.099609375 to 1.8984375
- norm_bias: bfloat16 [2048], replicated, may hold values from -3 to 3
- w_qkv: bfloat16 [2048, 3, 1024], P(None, None, 'tp'), may hold values from -10 to 10
- segment_ids: int32 [32768], P('req'), may hold values from 0 to 63, never falling along the last dimension, each value on 1 to 2048 neighbouring positions
- pack_lengths: int32 [2], replicated, may hold values from 16256 to 16384
- page_table: int32 [256, 2], P('req'), may hold values from 0 to 127, as said below
Outputs:
- context: bfloat16 [32768, 1024], P('req', 'tp')
- kv_cache: bfloat16 [512, 2, 128, 1024], P('req', None, None, 'tp')
The draws below stay inside these ranges and needn't reach their ends.
Inputs may be any that keep to these rules, and one draw needn't show every extreme that they name: `segment_ids`: never falling along the tokens; each id covers at most 2048 consecutive tokens and some id exactly 2048. `page_table`: row g holds the owning device and the slot of the g-th page of 128 tokens. Within each aligned group of 64 devices, the j-th page of every device goes the same number of devices forward, 1 to 8, into slot j, unless that passes the last device of the axis; then it stays on its own device in slot j + 2.
All inputs are finite; a program needn't handle non-finite values.
Results may differ from the reference program's by a relative error of at most 0.0099.
Values may be sent and summed in bfloat16 or wider, within the bound.
A program may use at most 64 MiB of HBM per device.

```python
import math
import jax
import jax.numpy as jnp
import numpy as np
from jax import lax

D = 2048
HEADS = 8
HD = 128
PAGE = 128
SEG_MAX = 2048
TOK_DEV = 256
HH = 1024
TOKENS = 32768
PACK_LEN = 16384
PACKS = 2
REACH = 8
SLOTS = 4
NPAGES = 256
N_REQ = 128


def draw_tokens(key, part):
    drawn_base = jax.random.truncated_normal(jax.random.fold_in(key, 1), -6.0, 6.0, (TOKENS, D), jnp.float32)
    column_scale = jnp.exp(jax.random.uniform(jax.random.fold_in(key, 3), (1, D), jnp.float32) * math.log(10.0))
    row_scale = jnp.exp(jax.random.uniform(jax.random.fold_in(key, 2), (TOKENS, 1), jnp.float32) * math.log(10.0))
    return (drawn_base * row_scale * column_scale).astype(jnp.bfloat16)


def draw_w_qkv(key, part):
    factor = D ** (-0.5)
    query_side = jax.random.truncated_normal(jax.random.fold_in(key, 1), -6.0, 6.0, (D, HH), jnp.float32) * factor
    key_side = jax.random.truncated_normal(jax.random.fold_in(key, 3), -6.0, 6.0, (D, HH), jnp.float32) * factor
    value_side = jax.random.truncated_normal(jax.random.fold_in(key, 4), -6.0, 6.0, (D, HH), jnp.float32) * factor
    return jnp.stack([query_side, key_side, value_side], axis=1).astype(jnp.bfloat16)


def draw_page_table(key, part):
    per_pack = PACK_LEN // TOK_DEV
    pages_dev = TOK_DEV // PAGE
    device_count = TOKENS // TOK_DEV
    forward = jax.random.randint(jax.random.fold_in(key, 11), (PACKS, pages_dev), 1, REACH + 1, jnp.int32)
    page_ids = jnp.arange(NPAGES, dtype=jnp.int32)
    device = page_ids // pages_dev
    column = page_ids % pages_dev
    pack_ids = device // per_pack
    forward_by = forward[pack_ids, column]
    goes_ahead = device + forward_by <= device_count - 1
    owner_ids = jnp.where(goes_ahead, device + forward_by, device)
    slot_ids = jnp.where(goes_ahead, column, column + pages_dev)
    return jnp.stack([owner_ids, slot_ids], axis=1).astype(jnp.int32)


def profile(amount, total, limit, skew):
    portions = [(1 << 20) // math.isqrt(rank ** skew) + 1 for rank in range(2, amount + 1)]
    rest, counts = total - limit - (amount - 1), [1] * (amount - 1)
    while rest > 0:
        free = [i for i in range(amount - 1) if counts[i] < limit]
        mass, left = sum([portions[i] for i in free]), rest
        for i in free:
            more = min(limit - counts[i], max(1, left * portions[i] // mass), rest)
            counts[i] = counts[i] + more
            rest = rest - more
    return np.array([limit] + counts)


def uneven(key, number_of, total, bound, skew):
    if number_of == 2:
        one = jax.random.randint(key, (), max(1, total - bound), min(bound, total - 1) + 1)
        return jnp.stack([one, total - one])
    tallies = jnp.asarray(profile(number_of, total, bound, skew), jnp.int32)
    pairs = (number_of - 1) // 2
    giver, receiver = tallies[1:1 + 2 * pairs:2], tallies[2:2 + 2 * pairs:2]
    slack = jnp.minimum(giver - 1, bound - receiver)
    moved = jax.random.randint(jax.random.fold_in(key, 1), (pairs,), 0, 1 << 20) % (slack + 1)
    tallies = tallies.at[1:1 + 2 * pairs:2].set(giver - moved).at[2:2 + 2 * pairs:2].set(receiver + moved)
    return tallies[jax.random.permutation(jax.random.fold_in(key, 2), number_of)]


def scatter_about(stream_key, extent, spread, limit, kind=jnp.bfloat16):
    entries = spread * jax.random.normal(stream_key, extent, jnp.float32)
    return jnp.clip(entries, min=-limit, max=limit).astype(kind)


def setup_inputs(seed: int = 0) -> dict:
    arg_keys = jax.random.split(jax.random.key(seed), 8)
    return {
        "tokens": draw_tokens(jax.random.fold_in(arg_keys[7], 71), 0),
        "norm_gain": jnp.clip(1.0 + 0.18 * jax.random.normal(arg_keys[1], (D,), jnp.float32), 0.099609375, 1.8984375).astype(jnp.bfloat16),
        "norm_bias": scatter_about(arg_keys[2], (D,), 0.5, 3.0),
        "w_qkv": draw_w_qkv(jax.random.fold_in(arg_keys[7], 71), 0),
        "segment_ids": jnp.searchsorted(jnp.cumsum(uneven(arg_keys[4], TOKENS // SEG_MAX * 4, TOKENS, SEG_MAX, 2)), jnp.arange(TOKENS), side="right").astype(jnp.int32),
        "pack_lengths": jax.random.randint(arg_keys[5], (PACKS,), PACK_LEN - TOK_DEV // 2, PACK_LEN + 1).astype(jnp.int32),
        "page_table": draw_page_table(jax.random.fold_in(arg_keys[7], 71), 0),
    }


def layer_norm(features, norm_gain, norm_bias):
    as_float = features.astype(jnp.float32)
    row_mean = lax.optimization_barrier(jnp.mean(as_float, axis=-1, keepdims=True))
    centred = as_float - row_mean
    variance = lax.optimization_barrier(jnp.mean(centred * centred, axis=-1, keepdims=True))
    scaled = centred * lax.rsqrt(variance + 1e-05)
    return (scaled * norm_gain.astype(jnp.float32) + norm_bias.astype(jnp.float32)).astype(jnp.bfloat16)

def reference(tokens, norm_gain, norm_bias, w_qkv, segment_ids, pack_lengths, page_table):
    normed = layer_norm(tokens, norm_gain, norm_bias)
    projected = jnp.dot(normed, w_qkv.reshape(D, 3 * HH), preferred_element_type=jnp.float32).reshape(TOKENS, 3, HH)
    positions = jnp.arange(TOKENS, dtype=jnp.int32)
    in_length = (positions % PACK_LEN < pack_lengths[positions // PACK_LEN])[:, None]
    queries = (projected[:, 0] * HD ** (-0.5)).astype(jnp.bfloat16)
    key_rows = jnp.where(in_length, projected[:, 1], 0.0).astype(jnp.bfloat16)
    value_rows = jnp.where(in_length, projected[:, 2], 0.0).astype(jnp.bfloat16)
    window = REACH * TOK_DEV
    padded_keys = jnp.concatenate([jnp.zeros((window, HH), jnp.bfloat16), key_rows], axis=0)
    padded_values = jnp.concatenate([jnp.zeros((window, HH), jnp.bfloat16), value_rows], axis=0)
    padded_ids = jnp.concatenate([jnp.full((window,), -1, jnp.int32), segment_ids.astype(jnp.int32)], axis=0)

    def attend_block(block_index):
        first = (block_index * TOK_DEV).astype(jnp.int32)
        query_part = lax.dynamic_slice_in_dim(queries, first, TOK_DEV, 0)
        query_ids = lax.dynamic_slice_in_dim(segment_ids.astype(jnp.int32), first, TOK_DEV, 0)
        key_part = lax.dynamic_slice_in_dim(padded_keys, first, window + TOK_DEV, 0)
        value_part = lax.dynamic_slice_in_dim(padded_values, first, window + TOK_DEV, 0)
        key_ids = lax.dynamic_slice_in_dim(padded_ids, first, window + TOK_DEV, 0)
        query_pos = first + jnp.arange(TOK_DEV, dtype=jnp.int32)
        key_pos = first - window + jnp.arange(window + TOK_DEV, dtype=jnp.int32)
        allowed = (key_pos >= 0)[None, :] & (key_pos[None, :] <= query_pos[:, None])
        allowed = allowed & (key_ids[None, :] == query_ids[:, None])
        allowed = allowed & ((key_pos // PACK_LEN)[None, :] == (query_pos // PACK_LEN)[:, None])
        query_heads = query_part.astype(jnp.float32).reshape(TOK_DEV, HEADS, HD)
        key_heads = key_part.astype(jnp.float32).reshape(window + TOK_DEV, HEADS, HD)
        value_heads = value_part.astype(jnp.float32).reshape(window + TOK_DEV, HEADS, HD)
        scores = jnp.einsum('qhd,khd->hqk', query_heads, key_heads)
        scores = jnp.where(allowed[None], scores, -1e+30)
        row_max = lax.optimization_barrier(jnp.max(scores, axis=2, keepdims=True))
        exp_scores = jnp.exp(scores - row_max)
        row_sum = lax.optimization_barrier(jnp.sum(exp_scores, axis=2, keepdims=True))
        probs_bf = (exp_scores / row_sum).astype(jnp.bfloat16)
        mixed = jnp.einsum('hqk,khd->qhd', probs_bf.astype(jnp.float32), value_heads)
        return mixed.reshape(TOK_DEV, HH)
    context_all = lax.map(attend_block, jnp.arange(TOKENS // TOK_DEV, dtype=jnp.int32)).reshape(TOKENS, HH)
    context = jnp.where(in_length, context_all, 0.0).astype(jnp.bfloat16)
    page_data = jnp.stack([key_rows.reshape(NPAGES, PAGE, HH), value_rows.reshape(NPAGES, PAGE, HH)], axis=1)
    target = (page_table[:, 0] * SLOTS + page_table[:, 1]).astype(jnp.int32)
    kv_cache = jnp.zeros((N_REQ * SLOTS, 2, PAGE, HH), jnp.bfloat16).at[target].set(page_data)
    return (context, kv_cache)
```

```python
import jax
import jax.numpy as jnp
from jax import lax
from jax.sharding import PartitionSpec as P

HD = 128
PAGE = 128
REACH = 8


def shifted(shard, axis, by):
    devices = lax.axis_size(axis)
    pairs = [(i, i + by) for i in range(devices) if 0 <= i + by < devices]
    return lax.ppermute(shard, axis, pairs)


def layer_norm(features, norm_gain, norm_bias):
    as_float = features.astype(jnp.float32)
    row_mean = jnp.mean(as_float, axis=-1, keepdims=True)
    centred = as_float - row_mean
    variance = jnp.mean(centred * centred, axis=-1, keepdims=True)
    scaled = centred * lax.rsqrt(variance + 1e-05)
    return (scaled * norm_gain.astype(jnp.float32) + norm_bias.astype(jnp.float32)).astype(
        jnp.bfloat16
    )


def block_scores(queries, key_block, allowed):
    raw_scores = jnp.einsum("qhd,khd->hqk", queries, key_block, preferred_element_type=jnp.float32)
    return jnp.where(allowed[None], raw_scores, -1e30)


def weigh_values(probs_part, value_block):
    return jnp.einsum("hqk,khd->qhd", probs_part, value_block, preferred_element_type=jnp.float32)


def per_device(tokens, norm_gain, norm_bias, w_qkv, segment_ids, pack_lengths, page_table):
    gathered = lax.all_gather(tokens, "tp", axis=1, tiled=True)
    normed = layer_norm(gathered, norm_gain, norm_bias)
    row_count = gathered.shape[0]
    local_width = w_qkv.shape[2]
    head_count = local_width // HD
    projected = jnp.dot(
        normed, w_qkv.reshape(w_qkv.shape[0], 3 * local_width), preferred_element_type=jnp.float32
    )
    projected = projected.reshape(row_count, 3, local_width)
    device_index = lax.axis_index("req")
    per_pack = lax.axis_size("req") // pack_lengths.shape[0]
    pack_id = device_index // per_pack
    offsets = device_index % per_pack * row_count + jnp.arange(row_count, dtype=jnp.int32)
    in_length = (offsets < pack_lengths[pack_id])[:, None]
    queries = (
        (projected[:, 0] * HD ** (-0.5)).astype(jnp.bfloat16).reshape(row_count, head_count, HD)
    )
    key_rows = jnp.where(in_length, projected[:, 1], 0.0).astype(jnp.bfloat16)
    value_rows = jnp.where(in_length, projected[:, 2], 0.0).astype(jnp.bfloat16)
    own_block = (key_rows, value_rows, segment_ids, page_table)
    blocks = [own_block]
    for distance in range(1, REACH + 1):
        blocks.append(shifted((key_rows, value_rows, segment_ids, page_table), "req", distance))
    causal = jnp.arange(row_count)[None, :] <= jnp.arange(row_count)[:, None]
    mask_list = []
    for distance in range(REACH + 1):
        source = device_index - distance
        same_pack = (source >= 0) & (source // per_pack == pack_id)
        allowed = same_pack & (blocks[distance][2][None, :] == segment_ids[:, None])
        if distance == 0:
            allowed = allowed & causal
        mask_list.append(allowed)
    key_list = [block_tuple[0].reshape(row_count, head_count, HD) for block_tuple in blocks]
    value_list = [block_tuple[1].reshape(row_count, head_count, HD) for block_tuple in blocks]
    scores = block_scores(
        queries, jnp.concatenate(key_list, axis=0), jnp.concatenate(mask_list, axis=1)
    )
    row_max = jnp.max(scores, axis=2, keepdims=True)
    exp_scores = jnp.exp(scores - row_max)
    row_sum = jnp.sum(exp_scores, axis=2, keepdims=True)
    probs_bf = (exp_scores / row_sum).astype(jnp.bfloat16)
    context = weigh_values(probs_bf, jnp.concatenate(value_list, axis=0))
    context = jnp.where(in_length, context.reshape(row_count, local_width), 0.0).astype(
        jnp.bfloat16
    )
    page_count = row_count // PAGE
    slot_count = 2 * page_count
    slot_range = jnp.arange(slot_count, dtype=jnp.int32)
    cache_sum = jnp.zeros((slot_count, 2, PAGE, local_width), jnp.float32)
    taken = jnp.zeros((slot_count, 1), jnp.bool_)
    for distance, block_tuple in enumerate(blocks):
        table_part = block_tuple[3]
        hit = (
            (table_part[:, 0] == device_index)[None, :]
            & (table_part[:, 1][None, :] == slot_range[:, None])
            & (device_index >= distance)
        )
        chosen = (hit & ~taken).astype(jnp.bfloat16)
        taken = taken | jnp.any(hit, axis=1, keepdims=True)
        stacked = jnp.stack([block_tuple[0], block_tuple[1]]).reshape(
            2, page_count, PAGE, local_width
        )
        cache_sum = cache_sum + jnp.einsum(
            "sj,cjpx->scpx", chosen, stacked, preferred_element_type=jnp.float32
        )
    kv_cache = cache_sum.astype(jnp.bfloat16)
    return (context, kv_cache)


def solution(mesh):
    return jax.shard_map(
        per_device,
        mesh=mesh,
        in_specs=(P("req", "tp"), P(), P(), P(None, None, "tp"), P("req"), P(), P("req", None)),
        out_specs=(P("req", "tp"), P("req", None, None, "tp")),
        check_vma=False,
    )
```

```python
import functools

import jax
import jax.numpy as jnp
from jax import lax
from jax.experimental import pallas as pl
from jax.experimental.pallas import tpu as pltpu
from jax.sharding import PartitionSpec as P

HD = 128
PAGE = 128
HALF = 64
REACH = 8
Z = 8
Y_LO = 4
NEG = -1e30
MESH = pl.DeviceIdType.MESH


def kernel(
    n_req,
    per_pack,
    tokens_hbm,
    gain_ref,
    bias_ref,
    w_hbm,
    ids_ref,
    lengths_ref,
    owner_ref,
    context_ref,
    cache_ref,
    w_buf,
    x_buf,
    relay_buf,
    normed_buf,
    q_buf,
    kv_buf,
    meta_buf,
    acc_buf,
    max_buf,
    sum_buf,
    w_sem,
    x_sem,
    own_send,
    own_recv,
    mate_send,
    mate_recv,
    far_send,
    far_recv,
    pass_send,
    pass_recv,
    meta_send,
    meta_recv,
    kv_send,
    kv_recv,
):
    req = lax.axis_index("req")
    tp = lax.axis_index("tp")
    slice_width = tokens_hbm.shape[1]
    width = w_hbm.shape[2]
    heads = width // HD
    y_lo = lax.rem(req // Z, Y_LO)
    y_hi = tp // 2
    core = lax.rem(tp, 2)

    def along_req(by):
        return (lax.rem(req + by + n_req, n_req), tp)

    def along_y(by):
        y = lax.rem(y_hi * Y_LO + y_lo + by + 2 * Y_LO, 2 * Y_LO)
        new_lo, new_hi = lax.rem(y, Y_LO), y // Y_LO
        return (req + (new_lo - y_lo) * Z, new_hi * 2 + core)

    mate = (req, tp + 1 - 2 * core)

    def copy_to(source, target, send, recv, device):
        return pltpu.make_async_remote_copy(
            src_ref=source,
            dst_ref=target,
            send_sem=send,
            recv_sem=recv,
            device_id=device,
            device_id_type=MESH,
        )

    def owner_of(j):
        hi, lo = j // 2, j % 2
        new_hi = 1 - y_hi if hi else y_hi
        new_core = 1 - core if lo else core
        return new_hi * 2 + new_core

    x_copy = pltpu.make_async_copy(tokens_hbm, x_buf.at[0], x_sem)
    x_copy.start()
    w_copies = []
    for j in range(4):
        rows = pl.ds(pl.multiple_of(owner_of(j) * slice_width, slice_width), slice_width)
        w_copy = pltpu.make_async_copy(
            w_hbm.at[:, rows, :],
            w_buf.at[:, pl.ds(j * slice_width, slice_width), :],
            w_sem.at[j],
        )
        w_copy.start()
        w_copies.append(w_copy)

    barrier = pltpu.get_barrier_semaphore()
    partners = [along_req(1), along_req(-1), along_req(REACH), along_req(-REACH)]
    partners += [along_y(1), along_y(-1), along_y(3), along_y(-3), mate]
    for partner in partners:
        pl.semaphore_signal(barrier, inc=1, device_id=partner, device_id_type=MESH)

    meta_buf[0, 0:2, :] = ids_ref[...]
    for page in range(2):
        meta_buf[0, 2 + page : 3 + page, :] = jnp.full((1, PAGE), owner_ref[page, 0], jnp.int32)
    cache_ref[...] = jnp.zeros_like(cache_ref)
    x_copy.wait()
    pl.semaphore_wait(barrier, len(partners))

    def rows_of(page, half):
        return pl.ds(page * PAGE + half * HALF, HALF)

    own_copies, mate_copies, pass_copies, far_copies = {}, {}, {}, {}
    for page in range(2):
        for half in range(2):
            own_copies[page, half] = copy_to(
                x_buf.at[0, rows_of(page, half), :],
                relay_buf.at[page, half],
                own_send.at[page, half],
                own_recv.at[page, half],
                along_y(1 if half == 0 else -1),
            )
            pass_copies[page, half] = copy_to(
                relay_buf.at[page, half],
                x_buf.at[2, rows_of(page, half), :],
                pass_send.at[page, half],
                pass_recv.at[page, half],
                along_y(3 if half == 0 else -3),
            )
            far_copies[page, half] = copy_to(
                x_buf.at[2, rows_of(page, half), :],
                x_buf.at[3, rows_of(page, half), :],
                far_send.at[page, half],
                far_recv.at[page, half],
                mate,
            )
        mate_copies[page] = copy_to(
            x_buf.at[0, pl.ds(page * PAGE, PAGE), :],
            x_buf.at[1, pl.ds(page * PAGE, PAGE), :],
            mate_send.at[page],
            mate_recv.at[page],
            mate,
        )

    def kv_forward(slot, page):
        return copy_to(
            kv_buf.at[slot, page],
            kv_buf.at[slot + 1, page],
            kv_send.at[slot, page],
            kv_recv.at[slot + 1, page],
            along_req(1),
        )

    def kv_backward(slot, page):
        return copy_to(
            kv_buf.at[slot, page],
            kv_buf.at[slot - 1, page],
            kv_send.at[slot, page],
            kv_recv.at[slot - 1, page],
            along_req(-1),
        )

    def kv_jump(page):
        return copy_to(
            kv_buf.at[0, page],
            kv_buf.at[REACH, page],
            kv_send.at[REACH + 1, page],
            kv_recv.at[REACH, page],
            along_req(REACH),
        )

    def kv_arrival(slot, page):
        return copy_to(
            kv_buf.at[slot, page],
            kv_buf.at[slot, page],
            kv_send.at[slot, page],
            kv_recv.at[slot, page],
            along_req(1),
        )

    def meta_copy(source, target, send, by):
        return copy_to(
            meta_buf.at[source],
            meta_buf.at[target],
            meta_send.at[send],
            meta_recv.at[target],
            along_req(by),
        )

    meta_copies = {0: meta_copy(0, 1, 0, 1), 9: meta_copy(0, REACH, 9, REACH)}
    for slot in range(1, 4):
        meta_copies[slot] = meta_copy(slot, slot + 1, slot, 1)
        meta_copies[9 - slot] = meta_copy(9 - slot, 8 - slot, 9 - slot, -1)
    meta_source = {1: 0, 2: 1, 3: 2, 4: 3, 8: 9, 7: 8, 6: 7, 5: 6}

    for page in range(2):
        for half in range(2):
            own_copies[page, half].start()
        mate_copies[page].start()
        if page == 0:
            meta_copies[0].start()
            meta_copies[9].start()

    def pass_on(page):
        for half in range(2):
            own_copies[page, half].wait_recv()
            pass_copies[page, half].start()

    def meta_on(step):
        for slot in (step, 9 - step):
            meta_copies[meta_source[slot]].wait_recv()
            meta_copies[slot].start()

    def share_far(page):
        for half in range(2):
            pass_copies[page, half].wait_recv()
            far_copies[page, half].start()

    pass_on(0)
    meta_on(1)
    pass_on(1)
    meta_on(2)

    pack = req // per_pack
    used = lengths_ref[pack]
    first_offset = lax.rem(req, per_pack) * (2 * PAGE)

    def project(page):
        share_far(page)
        mate_copies[page].wait_recv()
        for half in range(2):
            far_copies[page, half].wait_recv()
        if page == 0:
            for w_copy in w_copies:
                w_copy.wait()

        def normalise(i, carry):
            rows = pl.ds(pl.multiple_of(page * PAGE + i * 32, 32), 32)
            parts = [x_buf[j, rows, :].astype(jnp.float32) for j in range(4)]
            count = 4.0 * slice_width
            mean = sum(jnp.sum(part, axis=1, keepdims=True) for part in parts) / count
            parts = [part - mean for part in parts]
            variance = sum(jnp.sum(part * part, axis=1, keepdims=True) for part in parts) / count
            scale = lax.rsqrt(variance + 1e-05)
            for j in range(4):
                owner = owner_of(j)
                gain = gain_ref[owner].astype(jnp.float32)
                bias = bias_ref[owner].astype(jnp.float32)
                normed_buf[pl.ds(pl.multiple_of(i * 32, 32), 32), pl.ds(j * slice_width, slice_width)] = (
                    parts[j] * scale * gain + bias
                ).astype(jnp.bfloat16)
            return carry

        lax.fori_loop(0, PAGE // 32, normalise, 0)
        offsets = first_offset + page * PAGE + lax.broadcasted_iota(jnp.int32, (PAGE, width), 0)
        valid = offsets < used
        for kind in range(2):
            projected = jnp.dot(normed_buf[...], w_buf[1 + kind], preferred_element_type=jnp.float32)
            kv_buf[0, page, kind] = jnp.where(valid, projected, 0.0).astype(jnp.bfloat16)
        kv_forward(0, page).start()
        kv_jump(page).start()
        projected = jnp.dot(normed_buf[...], w_buf[0], preferred_element_type=jnp.float32)
        q_buf[pl.ds(page * PAGE, PAGE), :] = (projected * HD ** (-0.5)).astype(jnp.bfloat16)

    project(0)
    meta_on(3)
    project(1)
    for slot in (4, 5):
        meta_copies[meta_source[slot]].wait_recv()

    query_ids = []
    for page in range(2):
        as_rows = jnp.broadcast_to(ids_ref[page : page + 1, :].astype(jnp.float32), (PAGE, PAGE))
        query_ids.append(as_rows.T)
    query_ids = jnp.concatenate(query_ids, axis=0)
    query_ids = jnp.concatenate([query_ids, query_ids], axis=1)
    first_of_pack = pack * per_pack

    def attend(slot, own):
        key_ids = jnp.concatenate([meta_buf[slot, 0:1, :], meta_buf[slot, 1:2, :]], axis=1)
        if own:
            allowed = key_ids.astype(jnp.float32) == query_ids
            shape = (2 * PAGE, 2 * PAGE)
            allowed = allowed & (
                lax.broadcasted_iota(jnp.int32, shape, 1) <= lax.broadcasted_iota(jnp.int32, shape, 0)
            )
        else:
            key_ids = jnp.where(req - slot >= first_of_pack, key_ids, -1)
            allowed = key_ids.astype(jnp.float32) == query_ids
        for head in range(heads):
            lanes = pl.ds(head * HD, HD)
            keys = jnp.concatenate([kv_buf[slot, page, 0, :, lanes] for page in range(2)], axis=0)
            values = jnp.concatenate([kv_buf[slot, page, 1, :, lanes] for page in range(2)], axis=0)
            scores = lax.dot_general(
                q_buf[:, lanes], keys, (((1,), (1,)), ((), ())), preferred_element_type=jnp.float32
            )
            scores = jnp.where(allowed, scores, NEG)
            block_max = jnp.max(scores, axis=1, keepdims=True)
            if own:
                new_max = jnp.broadcast_to(block_max, (2 * PAGE, HD))
            else:
                old_max = max_buf[head]
                new_max = jnp.maximum(old_max, block_max)
                fade = jnp.exp(old_max - new_max)
            weights = jnp.exp(scores - jnp.concatenate([new_max, new_max], axis=1))
            block_sum = jnp.sum(weights, axis=1, keepdims=True)
            mixed = jnp.dot(weights.astype(jnp.bfloat16), values, preferred_element_type=jnp.float32)
            if own:
                sum_buf[head] = jnp.broadcast_to(block_sum, (2 * PAGE, HD))
                acc_buf[head] = mixed
            else:
                sum_buf[head] = sum_buf[head] * fade + block_sum
                acc_buf[head] = acc_buf[head] * fade + mixed
            max_buf[head] = new_max

    def keep_pages(slot):
        for page in range(2):
            row = slice(2 + page, 3 + page)
            mine = (meta_buf[slot, row, :] == req) & (req >= slot)
            for nearer in range(1, REACH):
                names_me = (meta_buf[nearer, row, :] == req) & (req >= nearer)
                mine = mine & ~(names_me & (nearer < slot))
            mine = jnp.where(mine, 1.0, 0.0)
            mine = jnp.broadcast_to(jnp.concatenate([mine] * heads, axis=1), (PAGE, width)) > 0.5
            for kind in range(2):
                kept = jnp.where(
                    mine,
                    kv_buf[slot, page, kind].astype(jnp.float32),
                    cache_ref[page, kind].astype(jnp.float32),
                )
                cache_ref[page, kind] = kept.astype(jnp.bfloat16)

    attend(0, True)
    for page in range(2):
        stays = jnp.where(meta_buf[0, 2 + page : 3 + page, :] == req, 1.0, 0.0)
        stays = jnp.broadcast_to(jnp.concatenate([stays] * heads, axis=1), (PAGE, width)) > 0.5
        for kind in range(2):
            kept = jnp.where(stays, kv_buf[0, page, kind].astype(jnp.float32), 0.0)
            cache_ref[2 + page, kind] = kept.astype(jnp.bfloat16)

    def step(i, carry):
        for page in range(2):
            kv_arrival(i, page).wait_recv()

            @pl.when(i < 4)
            def _():
                kv_forward(i, page).start()

            kv_arrival(9 - i, page).wait_recv()

            @pl.when(i < 4)
            def _():
                kv_backward(9 - i, page).start()

        def one(k, inner):
            slot = jnp.where(k == 0, i, 9 - i)
            attend(slot, False)
            keep_pages(slot)
            return inner

        lax.fori_loop(0, 2, one, 0)
        return carry

    lax.fori_loop(1, 5, step, 0)

    offsets = first_offset + lax.broadcasted_iota(jnp.int32, (2 * PAGE, HD), 0)
    for head in range(heads):
        context = acc_buf[head] / sum_buf[head]
        context_ref[:, pl.ds(head * HD, HD)] = jnp.where(offsets < used, context, 0.0).astype(jnp.bfloat16)

    for page in range(2):
        for half in range(2):
            own_copies[page, half].wait_send()
            pass_copies[page, half].wait_send()
            far_copies[page, half].wait_send()
        mate_copies[page].wait_send()
        kv_jump(page).wait_send()
        kv_forward(0, page).wait_send()
        for slot in range(1, 4):
            kv_forward(slot, page).wait_send()
            kv_backward(9 - slot, page).wait_send()
    for meta in meta_copies.values():
        meta.wait_send()


def per_device(tokens, norm_gain, norm_bias, w_qkv, segment_ids, pack_lengths, page_table):
    rows, slice_width = tokens.shape
    depth, _, width = w_qkv.shape
    n_req = lax.axis_size("req")
    per_pack = n_req // pack_lengths.shape[0]
    heads = width // HD
    vmem = pl.BlockSpec(memory_space=pltpu.VMEM)
    smem = pl.BlockSpec(memory_space=pltpu.SMEM)
    hbm = pl.BlockSpec(memory_space=pl.ANY)
    dma = pltpu.SemaphoreType.DMA
    return pl.pallas_call(
        functools.partial(kernel, n_req, per_pack),
        out_shape=(
            jax.ShapeDtypeStruct((rows, width), jnp.bfloat16),
            jax.ShapeDtypeStruct((4, 2, PAGE, width), jnp.bfloat16),
        ),
        in_specs=[hbm, vmem, vmem, hbm, vmem, smem, smem],
        out_specs=(vmem, vmem),
        scratch_shapes=[
            pltpu.VMEM((3, depth, width), jnp.bfloat16),
            pltpu.VMEM((4, rows, slice_width), jnp.bfloat16),
            pltpu.VMEM((2, 2, HALF, slice_width), jnp.bfloat16),
            pltpu.VMEM((PAGE, depth), jnp.bfloat16),
            pltpu.VMEM((rows, width), jnp.bfloat16),
            pltpu.VMEM((REACH + 1, 2, 2, PAGE, width), jnp.bfloat16),
            pltpu.VMEM((REACH + 1, 8, PAGE), jnp.int32),
            pltpu.VMEM((heads, rows, HD), jnp.float32),
            pltpu.VMEM((heads, rows, HD), jnp.float32),
            pltpu.VMEM((heads, rows, HD), jnp.float32),
            dma((4,)),
            dma,
            dma((2, 2)),
            dma((2, 2)),
            dma((2,)),
            dma((2,)),
            dma((2, 2)),
            dma((2, 2)),
            dma((2, 2)),
            dma((2, 2)),
            dma((10,)),
            dma((9,)),
            dma((10, 2)),
            dma((9, 2)),
        ],
        compiler_params=pltpu.CompilerParams(collective_id=0, has_side_effects=True),
    )(
        tokens,
        norm_gain.reshape(4, 1, slice_width),
        norm_bias.reshape(4, 1, slice_width),
        jnp.transpose(w_qkv, (1, 0, 2)),
        segment_ids.reshape(2, PAGE),
        pack_lengths,
        page_table,
    )


def solution(mesh):
    return jax.shard_map(
        per_device,
        mesh=mesh,
        in_specs=(P("req", "tp"), P(), P(), P(None, None, "tp"), P("req"), P(), P("req", None)),
        out_specs=(P("req", "tp"), P("req", None, None, "tp")),
        check_vma=False,
    )
```
